32 devices in a mesh: slab: 2 (over x), freq: 4 (over y, core), energy: 4 (over z).
Axes of the slice: x: 2, y: 2, z: 4, core: 2. Of those that a mesh axis runs over, the one named last changes fastest.
Arguments:
- lesser: bfloat16 [8, 4, 2, 512, 512], P('energy', 'slab'), may hold values from -6 to 6
- retarded: bfloat16 [8, 4, 2, 512, 512], P('energy', 'slab'), may hold values from -0.25 to 0.25
- coupling: bfloat16 [8, 512, 512], P('freq'), may hold values from -0.125 to 0.125
- occupations: float32 [8], P('freq'), may hold values from 0.1 to 3
- offsets: int32 [8], P('freq'), may hold values from 1 to 2
- intersection: float32 [4], P('slab'), may hold values from 0.2 to 0.6
Outputs:
- updated: float32 [8, 4, 2, 512, 512], P('energy', 'slab', None, 'freq')
The draws below stay inside these ranges and needn't reach their ends.
All inputs are finite; a program needn't handle non-finite values.
Results may differ from the reference program's by a relative error of at most 0.017.
Values may be sent and summed in bfloat16 or wider, within the bound.
A program may use at most 128 MiB of HBM per device.

```python
import math
import jax
import jax.numpy as jnp
from jax import lax

NO = 512
OFFMAX = 2
FQ_DEV = 2
ENERGIES = 8
FREQS = 8
SLABS = 4
N_FREQ = 4


def place_ends(drawn, own_key, least, top_value):
    index_at = [jax.random.randint(jax.random.fold_in(own_key, axis), (), 0, length) for axis, length in enumerate(drawn.shape)]
    widest = drawn.shape.index(max(drawn.shape))
    neighbour = index_at[:widest] + [(index_at[widest] + 1) % drawn.shape[widest]] + index_at[widest + 1:]
    return drawn.at[tuple(index_at)].set(least).at[tuple(neighbour)].set(top_value)


def levels(key, shape, cuts, low, top_value):
    def one(dim, shards_of):
        heights = jax.random.uniform(jax.random.fold_in(jax.random.fold_in(key, 6), dim), (shards_of,), jnp.float32, low / len(cuts), top_value / len(cuts))
        return jnp.repeat(jnp.exp(heights), shape[dim] // shards_of).reshape((-1,) + (1,) * (len(shape) - dim - 1))

    factor_of = one(*cuts[0])
    for cut in cuts[1:]:
        factor_of = factor_of * one(*cut)
    return factor_of


def gaussian(own_key, shape, spread, bound, cuts=(), kind=jnp.bfloat16):
    drawn = jax.random.normal(own_key, shape, jnp.float32) * spread
    if len(cuts) > 0:
        drawn = levels(own_key, shape, cuts, -0.22, 0.18) * drawn
    return jnp.clip(drawn, min=-bound, max=bound).astype(kind)


def setup_inputs(seed: int = 0) -> dict:
    splits = jax.random.split(jax.random.key(seed), 7)
    return {
        "lesser": gaussian(splits[0], (ENERGIES, SLABS, 2, NO, NO), 1.0, 6.0, ((0, 4), (1, 2))),
        "retarded": gaussian(splits[1], (ENERGIES, SLABS, 2, NO, NO), NO ** -0.5, 0.25, ((0, 4), (1, 2))),
        "coupling": gaussian(splits[2], (FREQS, NO, NO), (4 * NO) ** -0.5, 0.125, ((0, 4),)),
        "occupations": jnp.clip(jnp.exp(math.log(3.0) - 3.4011974 * jax.random.uniform(splits[3], (FREQS,), jnp.float32) ** levels(splits[3], (FREQS,), ((0, 4),), -0.2, 0.2)), 0.1, 3.0),
        "offsets": place_ends(jax.random.randint(splits[4], (FREQS,), 1, OFFMAX + 1), jax.random.fold_in(splits[4], 1), 1, OFFMAX).astype(jnp.int32),
        "intersection": jnp.clip(0.2 + 0.400000021 * jax.random.uniform(splits[5], (SLABS,), jnp.float32) ** levels(splits[5], (SLABS,), ((0, 2),), -0.2, 0.2), 0.2, 0.6),
    }


def reference(lesser, retarded, coupling, occupations, offsets, intersection):
    padded = jnp.pad(lesser, ((OFFMAX, OFFMAX), (0, 0), (0, 0), (0, 0), (0, 0)))
    group_coupling = coupling.reshape(N_FREQ, FQ_DEV, NO, NO)
    group_numbers = occupations.reshape(N_FREQ, FQ_DEV)
    group_shifts = offsets.reshape(N_FREQ, FQ_DEV)

    def energy_term(energy_index):
        def group_add(accumulated, group):
            weights, numbers, shifts = group
            lower_index = (energy_index + OFFMAX - shifts).astype(jnp.int32)
            upper_index = (energy_index + OFFMAX + shifts).astype(jnp.int32)
            lower_green = jnp.take(padded, lower_index, axis=0).astype(jnp.float32)
            upper_green = jnp.take(padded, upper_index, axis=0).astype(jnp.float32)
            scale = numbers[:, None, None, None, None]
            mixture = scale * lower_green + (scale + 1.0) * upper_green
            mixture = lax.optimization_barrier(mixture.astype(jnp.bfloat16)).astype(jnp.float32)
            weights_wide = weights.astype(jnp.float32)
            left_product = jnp.einsum('fij,fscjk->fscik', weights_wide, mixture)
            left_product = lax.optimization_barrier(left_product.astype(jnp.bfloat16)).astype(jnp.float32)
            sandwich = jnp.einsum('fscik,fmk->scim', left_product, weights_wide)
            rounded = lax.optimization_barrier(sandwich.astype(jnp.bfloat16)).astype(jnp.float32)
            return accumulated + rounded, None

        initial = jnp.zeros((SLABS, 2, NO, NO), jnp.float32)
        result, unused = lax.scan(group_add, initial, (group_coupling, group_numbers, group_shifts))
        return result

    self_energy = lax.map(energy_term, jnp.arange(ENERGIES, dtype=jnp.int32))
    self_half = lax.optimization_barrier(self_energy.astype(jnp.bfloat16)).astype(jnp.float32)
    beside = jnp.pad(self_half, ((0, 0), (1, 1), (0, 0), (0, 0), (0, 0)))
    combined = self_half + intersection[None, :, None, None, None] * (beside[:, :-2] + beside[:, 2:])
    combined = lax.optimization_barrier(combined.astype(jnp.bfloat16)).astype(jnp.float32)
    green = retarded.astype(jnp.float32)
    real_green = green[:, :, 0]
    imag_green = green[:, :, 1]
    real_self = combined[:, :, 0]
    imag_self = combined[:, :, 1]

    def by_transpose(left_side, right_side):
        return jnp.einsum('esij,eskj->esik', left_side, right_side)

    real_part = by_transpose(real_self, real_green) + by_transpose(imag_self, imag_green)
    imag_part = by_transpose(imag_self, real_green) - by_transpose(real_self, imag_green)
    product = jnp.stack([real_part, imag_part], axis=2)
    product = lax.optimization_barrier(product.astype(jnp.bfloat16)).astype(jnp.float32)
    real_product = product[:, :, 0]
    imag_product = product[:, :, 1]

    def plain_product(left_side, right_side):
        return jnp.einsum('esij,esjk->esik', left_side, right_side)

    out_real = plain_product(real_green, real_product) - plain_product(imag_green, imag_product)
    out_imag = plain_product(real_green, imag_product) + plain_product(imag_green, real_product)
    return jnp.stack([out_real, out_imag], axis=2)
```

```python
import functools
import jax
import jax.numpy as jnp
from jax import lax
from jax.experimental import pallas as pl
from jax.experimental.pallas import tpu as pltpu
from jax.sharding import PartitionSpec as P

OFFMAX = 2
MESH = pl.DeviceIdType.MESH
F32 = jnp.float32
BF16 = jnp.bfloat16


def with_halo(block, sides, width):
    for axis, dim in sides:
        count = lax.axis_size(axis)
        forward = [(i, i + 1) for i in range(count - 1)]
        backward = [(target, source) for source, target in forward]
        low = lax.ppermute(
            lax.slice_in_dim(block, block.shape[dim] - width, None, axis=dim), axis, forward
        )
        high = lax.ppermute(lax.slice_in_dim(block, 0, width, axis=dim), axis, backward)
        block = jnp.concatenate([low, block, high], axis=dim)
    return block


def general(lesser, retarded, coupling, occupations, offsets, intersection):
    freq_count = lax.axis_size("freq")
    row_count = lesser.shape[-1] // freq_count
    row_first = lax.axis_index("freq") * row_count
    padded = with_halo(lesser, (("energy", 0),), OFFMAX)
    energy_count = lesser.shape[0]
    positions = jnp.arange(energy_count, dtype=jnp.int32)[None, :] + OFFMAX
    lower_green = jnp.take(padded, positions - offsets[:, None], axis=0)
    upper_green = jnp.take(padded, positions + offsets[:, None], axis=0)
    scale = occupations[:, None, None, None, None, None]
    mixture = (
        scale * lower_green.astype(F32) + (scale + 1.0) * upper_green.astype(F32)
    ).astype(BF16)
    real_green = retarded[:, :, 0]
    imag_green = retarded[:, :, 1]
    real_rows = lax.dynamic_slice_in_dim(real_green, row_first, row_count, 2)
    imag_rows = lax.dynamic_slice_in_dim(imag_green, row_first, row_count, 2)
    left_product = jnp.einsum(
        "fri,fescij->fescrj", coupling, mixture, preferred_element_type=F32
    ).astype(BF16)
    self_energy = lax.psum_scatter(
        jnp.einsum(
            "fescrj,fkj->resck", left_product, coupling, preferred_element_type=F32
        ).astype(BF16),
        "freq",
        scatter_dimension=0,
        tiled=True,
    )
    beside_all = with_halo(self_energy, (("slab", 2),), 1)
    beside = beside_all[:, :, :-2].astype(F32) + beside_all[:, :, 2:].astype(F32)
    total = self_energy.astype(F32) + intersection[None, None, :, None, None] * beside
    combined = total.astype(BF16)
    real_self = combined[:, :, :, 0]
    imag_self = combined[:, :, :, 1]

    def by_transpose(left_side, right_side):
        return jnp.einsum("resj,eskj->resk", left_side, right_side, preferred_element_type=F32)

    real_part = by_transpose(real_self, real_green) + by_transpose(imag_self, imag_green)
    imag_part = by_transpose(imag_self, real_green) - by_transpose(real_self, imag_green)
    product = jnp.stack([real_part, imag_part], axis=3).astype(BF16)
    y_piece = lax.all_gather(product, "freq", axis=0, tiled=True)
    real_piece = y_piece[:, :, :, 0]
    imag_piece = y_piece[:, :, :, 1]

    def plain_product(left_side, right_side):
        return jnp.einsum("esrm,mesk->esrk", left_side, right_side, preferred_element_type=F32)

    out_real = plain_product(real_rows, real_piece) - plain_product(imag_rows, imag_piece)
    out_imag = plain_product(real_rows, imag_piece) + plain_product(imag_rows, real_piece)
    return jnp.stack([out_real, out_imag], axis=2)


def by_rows(a, b):
    return lax.dot_general(a, b, (((1,), (1,)), ((), ())), preferred_element_type=F32)


def kernel(
    chunks, slabs, energies,
    lesser, retarded, coupling, weights, beside_weight, out,
    own, low, high, c_buf, w_buf, r_buf, acc, half, near, far, comb,
    local_sem, send_sem, recv_sem,
):
    nf, size, _ = coupling.shape
    cut = size // chunks
    x, q, z = lax.axis_index("slab"), lax.axis_index("freq"), lax.axis_index("energy")
    y, core = q // 2, q % 2
    partner = {"freq": 2 * y + 1 - core}
    across = {"freq": 2 * (1 - y) + core}
    diagonal = {"freq": 2 * (1 - y) + 1 - core}
    has_low, has_high = z > 0, z < energies - 1
    below = {"energy": jnp.maximum(z - 1, 0)}
    above = {"energy": jnp.minimum(z + 1, energies - 1)}
    x_to = x + 2 * core - 1
    has_x = jnp.logical_and(x_to >= 0, x_to < slabs)
    beside = {"slab": jnp.clip(x_to, 0, slabs - 1), "freq": 2 * y + 1 - core}

    barrier = pltpu.get_barrier_semaphore()
    peers = [(None, partner), (None, across), (None, diagonal), (has_low, below), (has_high, above), (has_x, beside)]

    def under(condition, action):
        if condition is None:
            action()
        else:
            pl.when(condition)(action)

    for condition, peer in peers:
        under(condition, lambda peer=peer: pl.semaphore_signal(barrier, inc=1, device_id=peer, device_id_type=MESH))

    count = [0]

    def remote(src, dst, peer):
        n = count[0]
        count[0] += 1
        return pltpu.make_async_remote_copy(
            src_ref=src, dst_ref=dst, send_sem=send_sem.at[n], recv_sem=recv_sem.at[n],
            device_id=peer, device_id_type=MESH,
        )

    load_own = pltpu.make_async_copy(lesser.at[:, core, y], own, local_sem.at[0])
    load_c = pltpu.make_async_copy(coupling, c_buf.at[pl.ds(0, nf)], local_sem.at[1])
    load_w = pltpu.make_async_copy(weights, w_buf.at[pl.ds(0, nf)], local_sem.at[2])
    load_r = pltpu.make_async_copy(retarded, r_buf, local_sem.at[3])
    for load in (load_own, load_c, load_w, load_r):
        load.start()

    def zero(ref):
        ref[...] = jnp.zeros_like(ref)

    pl.when(jnp.logical_not(has_low))(lambda: zero(low))
    pl.when(jnp.logical_not(has_high))(lambda: zero(high))
    pl.when(jnp.logical_not(has_x))(lambda: zero(far))
    zero(acc)

    greeted = 3 + sum(condition.astype(jnp.int32) for condition in (has_low, has_high, has_x))
    pl.semaphore_wait(barrier, greeted)

    sent = []

    def go(copy, condition=None):
        under(condition, copy.start)
        sent.append((condition, copy))
        return copy

    w_in = [
        go(remote(weights, w_buf.at[pl.ds(slot * nf, nf)], peer))
        for slot, peer in ((1, partner), (2, across), (3, diagonal))
    ]
    ups, downs, c_across = [], [], []
    c_near = [go(remote(coupling.at[i], c_buf.at[nf + i], partner)) for i in range(nf)]
    for k in range(chunks):
        columns = pl.ds(k * cut, cut)
        ups.append(go(remote(lesser.at[:, core, y, :, columns], low.at[k], above), has_high))
        downs.append(go(remote(lesser.at[:, core, y, :, columns], high.at[k], below), has_low))
        if k == 0:
            c_across = [go(remote(coupling.at[i], c_buf.at[2 * nf + i], across)) for i in range(nf)]

    load_own.wait()
    load_c.wait()
    load_w.wait()
    for copy in w_in:
        copy.wait_recv()

    def terms(k, e):
        columns = slice(k * cut, (k + 1) * cut)
        if e == 0:
            return low.at[k, 1], low.at[k, 0], own.at[1, :, columns], high.at[k, 0]
        return own.at[0, :, columns], low.at[k, 1], high.at[k, 0], high.at[k, 1]

    def sandwich(k, e, first, last):
        columns = slice(k * cut, (k + 1) * cut)
        refs = terms(k, e)

        def body(f, carry):
            w = w_buf[f]
            mixed = w[0:1] * refs[0][...].astype(F32)
            for i in (1, 2, 3):
                mixed = mixed + w[i : i + 1] * refs[i][...].astype(F32)
            left = jnp.dot(c_buf[f], mixed.astype(BF16), preferred_element_type=F32).astype(BF16)
            acc[e] += by_rows(left, c_buf[f, :, columns])
            return carry

        lax.fori_loop(first, last, body, 0)

    def arrive(k):
        pl.when(has_low)(ups[k].wait_recv)
        pl.when(has_high)(downs[k].wait_recv)

    arrive(0)
    for copy in c_near:
        copy.wait_recv()
    sandwich(0, 0, 0, 2 * nf)
    sandwich(0, 1, 0, 2 * nf)
    c_far = []
    for i in range(nf):
        c_across[i].wait_recv()
        c_far.append(go(remote(c_buf.at[2 * nf + i], c_buf.at[3 * nf + i], partner)))
    for copy in c_far:
        copy.wait_recv()
    for e in range(2):
        sandwich(0, e, 2 * nf, 4 * nf)

    to_near, to_far = [], []

    def finish_self(e):
        half[e] = acc[e].astype(BF16)
        to_far.append(go(remote(half.at[e], far.at[e], beside), has_x))
        to_near.append(go(remote(half.at[e], near.at[e], partner)))

    for k in range(1, chunks):
        arrive(k)
        for e in range(2):
            sandwich(k, e, 0, 4 * nf)
            if k == chunks - 1:
                finish_self(e)

    comb_near, comb_across = [], []
    for e in range(2):
        to_near[e].wait_recv()
        pl.when(has_x)(to_far[e].wait_recv)
        around = near[e].astype(F32) + far[e].astype(F32)
        comb[e, 0] = (half[e].astype(F32) + beside_weight[core] * around).astype(BF16)
        comb_across.append(go(remote(comb.at[e, 0], comb.at[e, 2], across)))
        comb_near.append(go(remote(comb.at[e, 0], comb.at[e, 1], partner)))

    load_r.wait()
    rows = size // 4
    mine = pl.ds(pl.multiple_of(q * rows, rows), rows)
    for e in range(2):
        comb_near[e].wait_recv()
        comb_across[e].wait_recv()
        comb_far = go(remote(comb.at[e, 2], comb.at[e, 3], partner))
        for other in range(2):
            if other == 1:
                comb_far.wait_recv()
            s = core if other == 0 else 1 - core
            edge = jnp.concatenate([r_buf[e, s, 0, mine, :], r_buf[e, s, 1, mine, :]], axis=0)
            with_real = jnp.dot(edge, comb[e, 2 * y + other], preferred_element_type=F32)
            with_imag = jnp.dot(edge, comb[e, 2 * (1 - y) + other], preferred_element_type=F32)
            middle = jnp.concatenate(
                [with_real[:rows] - with_imag[rows:], with_imag[:rows] + with_real[rows:]], axis=0
            ).astype(BF16)
            by_real = by_rows(middle, r_buf[e, s, 0])
            by_imag = by_rows(middle, r_buf[e, s, 1])
            out[e, s, 0] = by_real[:rows] + by_imag[rows:]
            out[e, s, 1] = by_real[rows:] - by_imag[:rows]

    for condition, copy in sent:
        under(condition, copy.wait_send)


def fast(lesser, retarded, coupling, occupations, offsets, intersection):
    nf, size, _ = coupling.shape
    chunks = 2
    cut = size // chunks
    near = (offsets == 1).astype(F32)
    away = (offsets == 2).astype(F32)
    more = occupations + 1.0
    rows = jnp.stack([occupations * near, occupations * away, more * near, more * away], axis=1)
    weights = jnp.broadcast_to(jnp.tile(rows, (1, 2))[:, :, None], (nf, 8, cut))
    copies = 3 + 2 * nf + nf + 2 * chunks + 4 + 4 + 2
    anywhere = pl.BlockSpec(memory_space=pl.ANY)
    return pl.pallas_call(
        functools.partial(kernel, chunks, lax.axis_size("slab"), lax.axis_size("energy")),
        out_shape=jax.ShapeDtypeStruct((2, 2, 2, size // 4, size), F32),
        in_specs=[anywhere] * 4 + [pl.BlockSpec(memory_space=pltpu.SMEM)],
        out_specs=pl.BlockSpec(memory_space=pltpu.VMEM),
        scratch_shapes=[
            pltpu.VMEM((2, size, size), BF16),
            pltpu.VMEM((chunks, 2, size, cut), BF16),
            pltpu.VMEM((chunks, 2, size, cut), BF16),
            pltpu.VMEM((4 * nf, size, size), BF16),
            pltpu.VMEM((4 * nf, 8, cut), F32),
            pltpu.VMEM((2, 2, 2, size, size), BF16),
            pltpu.VMEM((2, size, size), F32),
            pltpu.VMEM((2, size, size), BF16),
            pltpu.VMEM((2, size, size), BF16),
            pltpu.VMEM((2, size, size), BF16),
            pltpu.VMEM((2, 4, size, size), BF16),
            pltpu.SemaphoreType.DMA((4,)),
            pltpu.SemaphoreType.DMA((copies,)),
            pltpu.SemaphoreType.DMA((copies,)),
        ],
        compiler_params=pltpu.CompilerParams(
            collective_id=0, has_side_effects=True, vmem_limit_bytes=60 << 20
        ),
    )(lesser, retarded, coupling, weights, intersection)


def solution(mesh):
    def shards(lesser, retarded, *rest):
        fits = (
            mesh.shape["freq"] == 4
            and lesser.shape[:2] == (2, 2)
            and lesser.shape[-1] % 512 == 0
            and rest[0].shape[0] * lesser.shape[-1] <= 1024
        )
        return (fast if fits else general)(lesser, retarded, *rest)

    return jax.shard_map(
        shards,
        mesh=mesh,
        in_specs=(
            P("energy", "slab", None, None, None),
            P("energy", "slab", None, None, None),
            P("freq", None, None),
            P("freq"),
            P("freq"),
            P("slab"),
        ),
        out_specs=P("energy", "slab", None, "freq", None),
        check_vma=False,
    )
```

```python
import functools
import jax
import jax.numpy as jnp
from jax import lax
from jax.experimental import pallas as pl
from jax.experimental.pallas import tpu as pltpu
from jax.sharding import PartitionSpec as P

OFFMAX = 2
UNROLL = 4
MESH = pl.DeviceIdType.MESH
F32 = jnp.float32
BF16 = jnp.bfloat16


def with_halo(block, sides, width):
    for axis, dim in sides:
        count = lax.axis_size(axis)
        forward = [(i, i + 1) for i in range(count - 1)]
        backward = [(target, source) for source, target in forward]
        low = lax.ppermute(
            lax.slice_in_dim(block, block.shape[dim] - width, None, axis=dim), axis, forward
        )
        high = lax.ppermute(lax.slice_in_dim(block, 0, width, axis=dim), axis, backward)
        block = jnp.concatenate([low, block, high], axis=dim)
    return block


def general(lesser, retarded, coupling, occupations, offsets, intersection):
    freq_count = lax.axis_size("freq")
    row_count = lesser.shape[-1] // freq_count
    row_first = lax.axis_index("freq") * row_count
    padded = with_halo(lesser, (("energy", 0),), OFFMAX)
    energy_count = lesser.shape[0]
    positions = jnp.arange(energy_count, dtype=jnp.int32)[None, :] + OFFMAX
    lower_green = jnp.take(padded, positions - offsets[:, None], axis=0)
    upper_green = jnp.take(padded, positions + offsets[:, None], axis=0)
    scale = occupations[:, None, None, None, None, None]
    mixture = (
        scale * lower_green.astype(F32) + (scale + 1.0) * upper_green.astype(F32)
    ).astype(BF16)
    real_green = retarded[:, :, 0]
    imag_green = retarded[:, :, 1]
    real_rows = lax.dynamic_slice_in_dim(real_green, row_first, row_count, 2)
    imag_rows = lax.dynamic_slice_in_dim(imag_green, row_first, row_count, 2)
    left_product = jnp.einsum(
        "fri,fescij->fescrj", coupling, mixture, preferred_element_type=F32
    ).astype(BF16)
    self_energy = lax.psum_scatter(
        jnp.einsum(
            "fescrj,fkj->resck", left_product, coupling, preferred_element_type=F32
        ).astype(BF16),
        "freq",
        scatter_dimension=0,
        tiled=True,
    )
    beside_all = with_halo(self_energy, (("slab", 2),), 1)
    beside = beside_all[:, :, :-2].astype(F32) + beside_all[:, :, 2:].astype(F32)
    total = self_energy.astype(F32) + intersection[None, None, :, None, None] * beside
    combined = total.astype(BF16)
    real_self = combined[:, :, :, 0]
    imag_self = combined[:, :, :, 1]

    def by_transpose(left_side, right_side):
        return jnp.einsum("resj,eskj->resk", left_side, right_side, preferred_element_type=F32)

    real_part = by_transpose(real_self, real_green) + by_transpose(imag_self, imag_green)
    imag_part = by_transpose(imag_self, real_green) - by_transpose(real_self, imag_green)
    product = jnp.stack([real_part, imag_part], axis=3).astype(BF16)
    y_piece = lax.all_gather(product, "freq", axis=0, tiled=True)
    real_piece = y_piece[:, :, :, 0]
    imag_piece = y_piece[:, :, :, 1]

    def plain_product(left_side, right_side):
        return jnp.einsum("esrm,mesk->esrk", left_side, right_side, preferred_element_type=F32)

    out_real = plain_product(real_rows, real_piece) - plain_product(imag_rows, imag_piece)
    out_imag = plain_product(real_rows, imag_piece) + plain_product(imag_rows, real_piece)
    return jnp.stack([out_real, out_imag], axis=2)


def by_rows(a, b):
    return lax.dot_general(a, b, (((1,), (1,)), ((), ())), preferred_element_type=F32)


def kernel(
    chunks, slabs, energies,
    lesser, retarded, coupling, numbers, shifts, beside_weight, out,
    own, low, high, c_buf, w_buf, r_buf, left_buf, acc, half, near, far, comb,
    local_sem, send_sem, recv_sem,
):
    nf, size, _ = coupling.shape
    cut = size // chunks
    x, q, z = lax.axis_index("slab"), lax.axis_index("freq"), lax.axis_index("energy")
    y, core = q // 2, q % 2
    partner = {"freq": 2 * y + 1 - core}
    across = {"freq": 2 * (1 - y) + core}
    diagonal = {"freq": 2 * (1 - y) + 1 - core}
    opposite = {"slab": 1 - x}
    has_low, has_high = z > 0, z < energies - 1
    below = {"energy": jnp.maximum(z - 1, 0)}
    above = {"energy": jnp.minimum(z + 1, energies - 1)}
    x_to = x + 2 * core - 1
    has_x = jnp.logical_and(x_to >= 0, x_to < slabs)
    beside = {"slab": jnp.clip(x_to, 0, slabs - 1), "freq": 2 * y + 1 - core}

    barrier = pltpu.get_barrier_semaphore()
    peers = [(None, partner), (None, across), (None, diagonal), (None, opposite), (has_low, below), (has_high, above), (has_x, beside)]

    def under(condition, action):
        if condition is None:
            action()
        else:
            pl.when(condition)(action)

    for condition, peer in peers:
        under(condition, lambda peer=peer: pl.semaphore_signal(barrier, inc=1, device_id=peer, device_id_type=MESH))

    count = [0]

    def remote(src, dst, peer):
        n = count[0]
        count[0] += 1
        return pltpu.make_async_remote_copy(
            src_ref=src, dst_ref=dst, send_sem=send_sem.at[n], recv_sem=recv_sem.at[n],
            device_id=peer, device_id_type=MESH,
        )

    load_own = pltpu.make_async_copy(lesser.at[:, core, y], own, local_sem.at[0])
    load_c = [
        pltpu.make_async_copy(
            coupling.at[i, :, pl.ds(k * cut, cut)],
            c_buf.at[k, :, pl.ds(i * cut, cut)],
            local_sem.at[3 + i * chunks + k],
        )
        for i in range(nf)
        for k in range(chunks)
    ]
    load_r = pltpu.make_async_copy(retarded, r_buf, local_sem.at[1])
    for load in [load_own, load_r] + load_c:
        load.start()

    for i in range(nf):
        number, shift = numbers[i], shifts[i]
        none = jnp.float32(0.0)
        row = [
            jnp.where(shift == 1, number, none),
            jnp.where(shift == 2, number, none),
            jnp.where(shift == 1, number + 1.0, none),
            jnp.where(shift == 2, number + 1.0, none),
        ]
        for j in range(8):
            w_buf[i, j : j + 1, :] = jnp.full((1, cut), row[j % 4], F32)

    def zero(ref):
        ref[...] = jnp.zeros_like(ref)

    pl.when(jnp.logical_not(has_low))(lambda: zero(low))
    pl.when(jnp.logical_not(has_high))(lambda: zero(high))
    pl.when(jnp.logical_not(has_x))(lambda: zero(far))

    greeted = 4 + sum(condition.astype(jnp.int32) for condition in (has_low, has_high, has_x))
    pl.semaphore_wait(barrier, greeted)

    sent = []

    def go(copy, condition=None):
        under(condition, copy.start)
        sent.append((condition, copy))
        return copy

    w_in = [
        go(remote(w_buf.at[pl.ds(0, nf)], w_buf.at[pl.ds(slot * nf, nf)], peer))
        for slot, peer in ((1, partner), (2, across), (3, diagonal))
    ]

    def part(slot, k):
        start = slot * cut
        return c_buf.at[k, :, pl.ds(start if isinstance(start, int) else pl.multiple_of(start, cut), cut)]

    ups, downs, c_across, c_near = [], [], [], []
    for k in range(chunks):
        columns = pl.ds(k * cut, cut)
        c_across.append(go(remote(coupling.at[x, :, columns], part(2 * nf + x, k), across)))
    for k in range(chunks):
        columns = pl.ds(k * cut, cut)
        for i in range(nf):
            c_near.append(go(remote(coupling.at[i, :, columns], part(nf + i, k), partner)))
        ups.append(go(remote(lesser.at[:, core, y, :, columns], low.at[k], above), has_high))
        downs.append(go(remote(lesser.at[:, core, y, :, columns], high.at[k], below), has_low))

    load_own.wait()
    for load in load_c:
        load.wait()
    for copy in w_in:
        copy.wait_recv()

    def terms(k, e):
        columns = slice(k * cut, (k + 1) * cut)
        if e == 0:
            return low.at[k, 1], low.at[k, 0], own.at[1, :, columns], high.at[k, 0]
        return own.at[0, :, columns], low.at[k, 1], high.at[k, 0], high.at[k, 1]

    def left_side(k, e, number, slot_of):
        refs = terms(k, e)

        def body(j, carry):
            f = slot_of(j)
            w = w_buf[f]
            mixed = w[0:1] * refs[0][...].astype(F32)
            for i in (1, 2, 3):
                mixed = mixed + w[i : i + 1] * refs[i][...].astype(F32)
            columns = pl.ds(pl.multiple_of(f * cut, cut), cut)
            whole = jnp.concatenate([c_buf[h, :, columns] for h in range(chunks)], axis=1)
            left = jnp.dot(whole, mixed.astype(BF16), preferred_element_type=F32)
            left_buf[e, :, columns] = left.astype(BF16)
            return carry

        lax.fori_loop(0, number, body, 0, unroll=UNROLL)

    def right_side(k, e):
        return by_rows(left_buf[e], c_buf[k])

    def arrive(k):
        pl.when(has_low)(ups[k].wait_recv)
        pl.when(has_high)(downs[k].wait_recv)

    relayed, c_far = [], []
    for k in range(chunks):
        c_across[k].wait_recv()
        relayed.append(go(remote(part(2 * nf + x, k), part(2 * nf + x, k), opposite)))
        c_far.append(go(remote(part(2 * nf + x, k), part(3 * nf + x, k), partner)))
    arrive(0)
    for copy in c_near:
        copy.wait_recv()
    for e in range(2):
        left_side(0, e, 2 * nf, lambda j: j)
    other_x = 1 - x
    c_rest = []
    for k in range(chunks):
        relayed[k].wait_recv()
        c_rest.append(go(remote(part(2 * nf + other_x, k), part(3 * nf + other_x, k), partner)))
    for copy in c_far + c_rest:
        copy.wait_recv()
    for e in range(2):
        left_side(0, e, 2 * nf, lambda j: 2 * nf + j)
        acc[e] = right_side(0, e)

    to_near, to_far = [], []

    def finish_self(e):
        half[e] = (acc[e] + right_side(chunks - 1, e)).astype(BF16)
        to_far.append(go(remote(half.at[e], far.at[e], beside), has_x))
        to_near.append(go(remote(half.at[e], near.at[e], partner)))

    for k in range(1, chunks - 1):
        arrive(k)
        for e in range(2):
            left_side(k, e, 4 * nf, lambda j: j)
            acc[e] += right_side(k, e)

    comb_across = [remote(comb.at[e, 0], comb.at[e, 2], across) for e in range(2)]
    comb_near = [remote(comb.at[e, 0], comb.at[e, 1], partner) for e in range(2)]
    comb_far = [remote(comb.at[e, 2], comb.at[e, 3], partner) for e in range(2)]

    def combine(e, with_far):
        to_near[e].wait_recv()
        around = near[e].astype(F32)
        if with_far:
            to_far[e].wait_recv()
            around = around + far[e].astype(F32)
        comb[e, 0] = (half[e].astype(F32) + beside_weight[core] * around).astype(BF16)
        comb_across[e].start()
        comb_near[e].start()

    alone = jnp.logical_not(has_x)
    last = chunks - 1
    arrive(last)
    left_side(last, 0, 4 * nf, lambda j: j)
    finish_self(0)
    left_side(last, 1, 4 * nf, lambda j: j)
    pl.when(alone)(lambda: combine(0, False))
    finish_self(1)
    pl.when(alone)(lambda: combine(1, False))
    pl.when(has_x)(lambda: combine(0, True))
    pl.when(has_x)(lambda: combine(1, True))

    load_r.wait()
    rows = size // 4
    mine = pl.ds(pl.multiple_of(q * rows, rows), rows)

    def pass_on(e):
        comb_across[e].wait_recv()
        comb_far[e].start()

    def take(e):
        comb_near[e].wait_recv()
        comb_far[e].wait_recv()

    for group in range(2):
        same = alone if group == 0 else has_x
        s = x if group == 0 else 1 - x
        other = jnp.where(same, 0, 1)
        for e in range(2):
            pl.when(same)(lambda e=e: pass_on(e))
            pl.when(jnp.logical_not(same))(lambda e=e: take(e))
            edge = jnp.concatenate([r_buf[e, s, 0, mine, :], r_buf[e, s, 1, mine, :]], axis=0)
            with_real = jnp.dot(edge, comb[e, 2 * y + other], preferred_element_type=F32)
            with_imag = jnp.dot(edge, comb[e, 2 * (1 - y) + other], preferred_element_type=F32)
            middle = jnp.concatenate(
                [with_real[:rows] - with_imag[rows:], with_imag[:rows] + with_real[rows:]], axis=0
            ).astype(BF16)
            by_real = by_rows(middle, r_buf[e, s, 0])
            by_imag = by_rows(middle, r_buf[e, s, 1])
            out[e, s, 0] = by_real[:rows] + by_imag[rows:]
            out[e, s, 1] = by_real[rows:] - by_imag[:rows]

    for copy in comb_across + comb_near + comb_far:
        copy.wait_send()
    for condition, copy in sent:
        under(condition, copy.wait_send)


def fast(lesser, retarded, coupling, occupations, offsets, intersection):
    nf, size, _ = coupling.shape
    chunks = 2
    cut = size // chunks
    copies = 3 + (nf + 6) * chunks + 10
    anywhere = pl.BlockSpec(memory_space=pl.ANY)
    return pl.pallas_call(
        functools.partial(kernel, chunks, lax.axis_size("slab"), lax.axis_size("energy")),
        out_shape=jax.ShapeDtypeStruct((2, 2, 2, size // 4, size), F32),
        in_specs=[anywhere] * 3 + [pl.BlockSpec(memory_space=pltpu.SMEM)] * 3,
        out_specs=pl.BlockSpec(memory_space=pltpu.VMEM),
        scratch_shapes=[
            pltpu.VMEM((2, size, size), BF16),
            pltpu.VMEM((chunks, 2, size, cut), BF16),
            pltpu.VMEM((chunks, 2, size, cut), BF16),
            pltpu.VMEM((chunks, size, 4 * nf * cut), BF16),
            pltpu.VMEM((4 * nf, 8, cut), F32),
            pltpu.VMEM((2, 2, 2, size, size), BF16),
            pltpu.VMEM((2, size, 4 * nf * cut), BF16),
            pltpu.VMEM((2, size, size), F32),
            pltpu.VMEM((2, size, size), BF16),
            pltpu.VMEM((2, size, size), BF16),
            pltpu.VMEM((2, size, size), BF16),
            pltpu.VMEM((2, 4, size, size), BF16),
            pltpu.SemaphoreType.DMA((3 + nf * chunks,)),
            pltpu.SemaphoreType.DMA((copies,)),
            pltpu.SemaphoreType.DMA((copies,)),
        ],
        compiler_params=pltpu.CompilerParams(
            collective_id=0, has_side_effects=True, vmem_limit_bytes=60 << 20
        ),
    )(lesser, retarded, coupling, occupations, offsets, intersection)


def solution(mesh):
    def shards(lesser, retarded, *rest):
        fits = (
            (mesh.shape["slab"], mesh.shape["freq"]) == (2, 4)
            and lesser.shape[:2] == (2, 2)
            and lesser.shape[-1] == 512
            and rest[0].shape[0] == 2
        )
        return (fast if fits else general)(lesser, retarded, *rest)

    return jax.shard_map(
        shards,
        mesh=mesh,
        in_specs=(
            P("energy", "slab", None, None, None),
            P("energy", "slab", None, None, None),
            P("freq", None, None),
            P("freq"),
            P("freq"),
            P("slab"),
        ),
        out_specs=P("energy", "slab", None, "freq", None),
        check_vma=False,
    )
```

```python
import functools
import jax
import jax.numpy as jnp
from jax import lax
from jax.experimental import pallas as pl
from jax.experimental.pallas import tpu as pltpu
from jax.sharding import PartitionSpec as P

OFFMAX = 2
UNROLL = 8
MESH = pl.DeviceIdType.MESH
F32 = jnp.float32
BF16 = jnp.bfloat16


def with_halo(block, sides, width):
    for axis, dim in sides:
        count = lax.axis_size(axis)
        forward = [(i, i + 1) for i in range(count - 1)]
        backward = [(target, source) for source, target in forward]
        low = lax.ppermute(
            lax.slice_in_dim(block, block.shape[dim] - width, None, axis=dim), axis, forward
        )
        high = lax.ppermute(lax.slice_in_dim(block, 0, width, axis=dim), axis, backward)
        block = jnp.concatenate([low, block, high], axis=dim)
    return block


def general(lesser, retarded, coupling, occupations, offsets, intersection):
    freq_count = lax.axis_size("freq")
    row_count = lesser.shape[-1] // freq_count
    row_first = lax.axis_index("freq") * row_count
    padded = with_halo(lesser, (("energy", 0),), OFFMAX)
    energy_count = lesser.shape[0]
    positions = jnp.arange(energy_count, dtype=jnp.int32)[None, :] + OFFMAX
    lower_green = jnp.take(padded, positions - offsets[:, None], axis=0)
    upper_green = jnp.take(padded, positions + offsets[:, None], axis=0)
    scale = occupations[:, None, None, None, None, None]
    mixture = (
        scale * lower_green.astype(F32) + (scale + 1.0) * upper_green.astype(F32)
    ).astype(BF16)
    real_green = retarded[:, :, 0]
    imag_green = retarded[:, :, 1]
    real_rows = lax.dynamic_slice_in_dim(real_green, row_first, row_count, 2)
    imag_rows = lax.dynamic_slice_in_dim(imag_green, row_first, row_count, 2)
    left_product = jnp.einsum(
        "fri,fescij->fescrj", coupling, mixture, preferred_element_type=F32
    ).astype(BF16)
    self_energy = lax.psum_scatter(
        jnp.einsum(
            "fescrj,fkj->resck", left_product, coupling, preferred_element_type=F32
        ).astype(BF16),
        "freq",
        scatter_dimension=0,
        tiled=True,
    )
    beside_all = with_halo(self_energy, (("slab", 2),), 1)
    beside = beside_all[:, :, :-2].astype(F32) + beside_all[:, :, 2:].astype(F32)
    total = self_energy.astype(F32) + intersection[None, None, :, None, None] * beside
    combined = total.astype(BF16)
    real_self = combined[:, :, :, 0]
    imag_self = combined[:, :, :, 1]

    def by_transpose(left_side, right_side):
        return jnp.einsum("resj,eskj->resk", left_side, right_side, preferred_element_type=F32)

    real_part = by_transpose(real_self, real_green) + by_transpose(imag_self, imag_green)
    imag_part = by_transpose(imag_self, real_green) - by_transpose(real_self, imag_green)
    product = jnp.stack([real_part, imag_part], axis=3).astype(BF16)
    y_piece = lax.all_gather(product, "freq", axis=0, tiled=True)
    real_piece = y_piece[:, :, :, 0]
    imag_piece = y_piece[:, :, :, 1]

    def plain_product(left_side, right_side):
        return jnp.einsum("esrm,mesk->esrk", left_side, right_side, preferred_element_type=F32)

    out_real = plain_product(real_rows, real_piece) - plain_product(imag_rows, imag_piece)
    out_imag = plain_product(real_rows, imag_piece) + plain_product(imag_rows, real_piece)
    return jnp.stack([out_real, out_imag], axis=2)


def by_rows(a, b):
    return lax.dot_general(a, b, (((1,), (1,)), ((), ())), preferred_element_type=F32)


def kernel(
    chunks, slabs, energies,
    lesser, retarded, coupling, numbers, shifts, beside_weight, out,
    own, low, high, c_buf, w_buf, r_buf, left_buf, acc, half, near, far, comb, result,
    store_sem, local_sem, send_sem, recv_sem,
):
    nf, size, _ = coupling.shape
    cut = size // chunks
    x, q, z = lax.axis_index("slab"), lax.axis_index("freq"), lax.axis_index("energy")
    y, core = q // 2, q % 2
    partner = {"freq": 2 * y + 1 - core}
    across = {"freq": 2 * (1 - y) + core}
    diagonal = {"freq": 2 * (1 - y) + 1 - core}
    opposite = {"slab": 1 - x}
    has_low, has_high = z > 0, z < energies - 1
    below = {"energy": jnp.maximum(z - 1, 0)}
    above = {"energy": jnp.minimum(z + 1, energies - 1)}
    x_to = x + 2 * core - 1
    has_x = jnp.logical_and(x_to >= 0, x_to < slabs)
    beside = {"slab": jnp.clip(x_to, 0, slabs - 1), "freq": 2 * y + 1 - core}

    barrier = pltpu.get_barrier_semaphore()
    peers = [(None, partner), (None, across), (None, diagonal), (None, opposite), (has_low, below), (has_high, above), (has_x, beside)]

    def under(condition, action):
        if condition is None:
            action()
        else:
            pl.when(condition)(action)

    for condition, peer in peers:
        under(condition, lambda peer=peer: pl.semaphore_signal(barrier, inc=1, device_id=peer, device_id_type=MESH))

    count = [0]

    def remote(src, dst, peer):
        n = count[0]
        count[0] += 1
        return pltpu.make_async_remote_copy(
            src_ref=src, dst_ref=dst, send_sem=send_sem.at[n], recv_sem=recv_sem.at[n],
            device_id=peer, device_id_type=MESH,
        )

    load_own = pltpu.make_async_copy(lesser.at[:, core, y], own, local_sem.at[0])
    load_c = [
        pltpu.make_async_copy(
            coupling.at[i, :, pl.ds(k * cut, cut)],
            c_buf.at[k, :, pl.ds(i * cut, cut)],
            local_sem.at[3 + i * chunks + k],
        )
        for i in range(nf)
        for k in range(chunks)
    ]
    load_r = pltpu.make_async_copy(retarded, r_buf, local_sem.at[1])
    for load in [load_own] + load_c:
        load.start()

    for i in range(nf):
        number, shift = numbers[i], shifts[i]
        none = jnp.float32(0.0)
        row = [
            jnp.where(shift == 1, number, none),
            jnp.where(shift == 2, number, none),
            jnp.where(shift == 1, number + 1.0, none),
            jnp.where(shift == 2, number + 1.0, none),
        ]
        for j in range(8):
            w_buf[i, j : j + 1, :] = jnp.full((1, cut), row[j % 4], F32)

    def zero(ref):
        ref[...] = jnp.zeros_like(ref)

    pl.when(jnp.logical_not(has_low))(lambda: zero(low))
    pl.when(jnp.logical_not(has_high))(lambda: zero(high))

    greeted = 4 + sum(condition.astype(jnp.int32) for condition in (has_low, has_high, has_x))
    pl.semaphore_wait(barrier, greeted)

    sent = []

    def go(copy, condition=None):
        under(condition, copy.start)
        sent.append((condition, copy))
        return copy

    w_in = [
        go(remote(w_buf.at[pl.ds(0, nf)], w_buf.at[pl.ds(slot * nf, nf)], peer))
        for slot, peer in ((1, partner), (2, across), (3, diagonal))
    ]

    def part(slot, k):
        start = slot * cut
        return c_buf.at[k, :, pl.ds(start if isinstance(start, int) else pl.multiple_of(start, cut), cut)]

    ups, downs, c_across, c_near = [], [], [], []
    for k in range(chunks):
        columns = pl.ds(k * cut, cut)
        c_across.append(go(remote(coupling.at[x, :, columns], part(2 * nf + x, k), across)))
    for k in range(chunks):
        columns = pl.ds(k * cut, cut)
        for i in range(nf):
            c_near.append(go(remote(coupling.at[i, :, columns], part(nf + i, k), partner)))
        ups.append(go(remote(lesser.at[:, core, y, :, columns], low.at[k], above), has_high))
        downs.append(go(remote(lesser.at[:, core, y, :, columns], high.at[k], below), has_low))

    load_r.start()
    load_own.wait()
    for load in load_c:
        load.wait()
    for copy in w_in:
        copy.wait_recv()

    def terms(k, e):
        columns = slice(k * cut, (k + 1) * cut)
        if e == 0:
            return low.at[k, 1], low.at[k, 0], own.at[1, :, columns], high.at[k, 0]
        return own.at[0, :, columns], low.at[k, 1], high.at[k, 0], high.at[k, 1]

    def left_side(k, e, number, slot_of):
        refs = terms(k, e)

        def body(j, carry):
            f = slot_of(j)
            w = w_buf[f]
            mixed = w[0:1] * refs[0][...].astype(F32)
            for i in (1, 2, 3):
                mixed = mixed + w[i : i + 1] * refs[i][...].astype(F32)
            columns = pl.ds(pl.multiple_of(f * cut, cut), cut)
            whole = jnp.concatenate([c_buf[h, :, columns] for h in range(chunks)], axis=1)
            left = jnp.dot(whole, mixed.astype(BF16), preferred_element_type=F32)
            left_buf[e, :, columns] = left.astype(BF16)
            return carry

        lax.fori_loop(0, number, body, 0, unroll=min(UNROLL, number))

    def right_side(k, e):
        return by_rows(left_buf[e], c_buf[k])

    def arrive(k):
        pl.when(has_low)(ups[k].wait_recv)
        pl.when(has_high)(downs[k].wait_recv)

    relayed, c_far = [], []
    for k in range(chunks):
        c_across[k].wait_recv()
        relayed.append(go(remote(part(2 * nf + x, k), part(2 * nf + x, k), opposite)))
        c_far.append(go(remote(part(2 * nf + x, k), part(3 * nf + x, k), partner)))
    arrive(0)
    for copy in c_near:
        copy.wait_recv()
    for e in range(2):
        left_side(0, e, 2 * nf, lambda j: j)
    other_x = 1 - x
    c_rest = []
    for k in range(chunks):
        relayed[k].wait_recv()
        c_rest.append(go(remote(part(2 * nf + other_x, k), part(3 * nf + other_x, k), partner)))
    for copy in c_far + c_rest:
        copy.wait_recv()
    for e in range(2):
        left_side(0, e, 2 * nf, lambda j: 2 * nf + j)
        acc[e] = right_side(0, e)

    for k in range(1, chunks - 1):
        arrive(k)
        for e in range(2):
            left_side(k, e, 4 * nf, lambda j: j)
            acc[e] += right_side(k, e)

    pairs = [(e, h) for e in range(2) for h in range(2)]
    to_far = {p: remote(half.at[p], far.at[p], beside) for p in pairs}
    to_near = {p: remote(half.at[p], near.at[p], partner) for p in pairs}
    comb_across = {(e, h): remote(comb.at[e, 0, h], comb.at[e, 2, h], across) for e, h in pairs}
    comb_near = {(e, h): remote(comb.at[e, 0, h], comb.at[e, 1, h], partner) for e, h in pairs}
    comb_far = {(e, h): remote(comb.at[e, 2, h], comb.at[e, 3, h], partner) for e, h in pairs}
    last = chunks - 1
    middle_column = size // 2

    def finish_self(e, h):
        columns = slice(h * middle_column, (h + 1) * middle_column)
        total = acc[e, :, columns] + by_rows(left_buf[e], c_buf[last, columns, :])
        half[e, h] = total.astype(BF16)
        go(to_far[e, h], has_x)
        go(to_near[e, h])

    def combine(e, h, with_far):
        to_near[e, h].wait_recv()
        around = near[e, h].astype(F32)
        if with_far:
            to_far[e, h].wait_recv()
            around = around + far[e, h].astype(F32)
        comb[e, 0, h] = (half[e, h].astype(F32) + beside_weight[core] * around).astype(BF16)
        comb_across[e, h].start()
        comb_near[e, h].start()

    alone = jnp.logical_not(has_x)

    def combine_alone(e, h):
        pl.when(alone)(lambda: combine(e, h, False))

    arrive(last)
    left_side(last, 0, 4 * nf, lambda j: j)
    finish_self(0, 0)
    finish_self(0, 1)
    combine_alone(0, 0)
    left_side(last, 1, 4 * nf, lambda j: j)
    combine_alone(0, 1)
    finish_self(1, 0)
    finish_self(1, 1)
    combine_alone(1, 0)
    combine_alone(1, 1)
    for e, h in pairs:
        pl.when(has_x)(lambda e=e, h=h: combine(e, h, True))

    load_r.wait()
    rows = size // 4
    mine = pl.ds(pl.multiple_of(q * rows, rows), rows)

    def pass_on(e):
        for h in range(2):
            comb_across[e, h].wait_recv()
            comb_far[e, h].start()

    def take(e):
        for h in range(2):
            comb_near[e, h].wait_recv()
            comb_far[e, h].wait_recv()

    def whole_sum(e, slot):
        return jnp.concatenate([comb[e, slot, 0], comb[e, slot, 1]], axis=1)

    stores = []

    for group in range(2):
        same = alone if group == 0 else has_x
        s = x if group == 0 else 1 - x
        other = jnp.where(same, 0, 1)
        for e in range(2):
            pl.when(same)(lambda e=e: pass_on(e))
            pl.when(jnp.logical_not(same))(lambda e=e: take(e))
            edge = jnp.concatenate([r_buf[e, s, 0, mine, :], r_buf[e, s, 1, mine, :]], axis=0)
            with_real = jnp.dot(edge, whole_sum(e, 2 * y + other), preferred_element_type=F32)
            with_imag = jnp.dot(edge, whole_sum(e, 2 * (1 - y) + other), preferred_element_type=F32)
            middle = jnp.concatenate(
                [with_real[:rows] - with_imag[rows:], with_imag[:rows] + with_real[rows:]], axis=0
            ).astype(BF16)
            by_real = by_rows(middle, r_buf[e, s, 0])
            by_imag = by_rows(middle, r_buf[e, s, 1])
            result[e, group, 0] = by_real[:rows] + by_imag[rows:]
            result[e, group, 1] = by_real[rows:] - by_imag[:rows]
            store = pltpu.make_async_copy(result.at[e, group], out.at[e, s], store_sem.at[e, group])
            store.start()
            stores.append(store)

    for copies in (comb_across, comb_near, comb_far):
        for p in pairs:
            copies[p].wait_send()
    for store in stores:
        store.wait()
    for condition, copy in sent:
        under(condition, copy.wait_send)


def fast(lesser, retarded, coupling, occupations, offsets, intersection):
    nf, size, _ = coupling.shape
    chunks = 2
    cut = size // chunks
    copies = 3 + (nf + 6) * chunks + 20
    anywhere = pl.BlockSpec(memory_space=pl.ANY)
    return pl.pallas_call(
        functools.partial(kernel, chunks, lax.axis_size("slab"), lax.axis_size("energy")),
        out_shape=jax.ShapeDtypeStruct((2, 2, 2, size // 4, size), F32),
        in_specs=[anywhere] * 3 + [pl.BlockSpec(memory_space=pltpu.SMEM)] * 3,
        out_specs=anywhere,
        scratch_shapes=[
            pltpu.VMEM((2, size, size), BF16),
            pltpu.VMEM((chunks, 2, size, cut), BF16),
            pltpu.VMEM((chunks, 2, size, cut), BF16),
            pltpu.VMEM((chunks, size, 4 * nf * cut), BF16),
            pltpu.VMEM((4 * nf, 8, cut), F32),
            pltpu.VMEM((2, 2, 2, size, size), BF16),
            pltpu.VMEM((2, size, 4 * nf * cut), BF16),
            pltpu.VMEM((2, size, size), F32),
            pltpu.VMEM((2, 2, size, size // 2), BF16),
            pltpu.VMEM((2, 2, size, size // 2), BF16),
            pltpu.VMEM((2, 2, size, size // 2), BF16),
            pltpu.VMEM((2, 4, 2, size, size // 2), BF16),
            pltpu.VMEM((2, 2, 2, size // 4, size), F32),
            pltpu.SemaphoreType.DMA((2, 2)),
            pltpu.SemaphoreType.DMA((3 + nf * chunks,)),
            pltpu.SemaphoreType.DMA((copies,)),
            pltpu.SemaphoreType.DMA((copies,)),
        ],
        compiler_params=pltpu.CompilerParams(
            collective_id=0, has_side_effects=True, vmem_limit_bytes=60 << 20
        ),
    )(lesser, retarded, coupling, occupations, offsets, intersection)


def solution(mesh):
    def shards(lesser, retarded, *rest):
        fits = (
            (mesh.shape["slab"], mesh.shape["freq"]) == (2, 4)
            and lesser.shape[:2] == (2, 2)
            and lesser.shape[-1] == 512
            and rest[0].shape[0] == 2
        )
        return (fast if fits else general)(lesser, retarded, *rest)

    return jax.shard_map(
        shards,
        mesh=mesh,
        in_specs=(
            P("energy", "slab", None, None, None),
            P("energy", "slab", None, None, None),
            P("freq", None, None),
            P("freq"),
            P("freq"),
            P("slab"),
        ),
        out_specs=P("energy", "slab", None, "freq", None),
        check_vma=False,
    )
```

```python
import functools
import jax
import jax.numpy as jnp
from jax import lax
from jax.experimental import pallas as pl
from jax.experimental.pallas import tpu as pltpu
from jax.sharding import PartitionSpec as P

OFFMAX = 2
UNROLL = 8
MESH = pl.DeviceIdType.MESH
F32 = jnp.float32
BF16 = jnp.bfloat16


def with_halo(block, sides, width):
    for axis, dim in sides:
        count = lax.axis_size(axis)
        forward = [(i, i + 1) for i in range(count - 1)]
        backward = [(target, source) for source, target in forward]
        low = lax.ppermute(
            lax.slice_in_dim(block, block.shape[dim] - width, None, axis=dim), axis, forward
        )
        high = lax.ppermute(lax.slice_in_dim(block, 0, width, axis=dim), axis, backward)
        block = jnp.concatenate([low, block, high], axis=dim)
    return block


def general(lesser, retarded, coupling, occupations, offsets, intersection):
    freq_count = lax.axis_size("freq")
    row_count = lesser.shape[-1] // freq_count
    row_first = lax.axis_index("freq") * row_count
    padded = with_halo(lesser, (("energy", 0),), OFFMAX)
    energy_count = lesser.shape[0]
    positions = jnp.arange(energy_count, dtype=jnp.int32)[None, :] + OFFMAX
    lower_green = jnp.take(padded, positions - offsets[:, None], axis=0)
    upper_green = jnp.take(padded, positions + offsets[:, None], axis=0)
    scale = occupations[:, None, None, None, None, None]
    mixture = (
        scale * lower_green.astype(F32) + (scale + 1.0) * upper_green.astype(F32)
    ).astype(BF16)
    real_green = retarded[:, :, 0]
    imag_green = retarded[:, :, 1]
    real_rows = lax.dynamic_slice_in_dim(real_green, row_first, row_count, 2)
    imag_rows = lax.dynamic_slice_in_dim(imag_green, row_first, row_count, 2)
    left_product = jnp.einsum(
        "fri,fescij->fescrj", coupling, mixture, preferred_element_type=F32
    ).astype(BF16)
    self_energy = lax.psum_scatter(
        jnp.einsum(
            "fescrj,fkj->resck", left_product, coupling, preferred_element_type=F32
        ).astype(BF16),
        "freq",
        scatter_dimension=0,
        tiled=True,
    )
    beside_all = with_halo(self_energy, (("slab", 2),), 1)
    beside = beside_all[:, :, :-2].astype(F32) + beside_all[:, :, 2:].astype(F32)
    total = self_energy.astype(F32) + intersection[None, None, :, None, None] * beside
    combined = total.astype(BF16)
    real_self = combined[:, :, :, 0]
    imag_self = combined[:, :, :, 1]

    def by_transpose(left_side, right_side):
        return jnp.einsum("resj,eskj->resk", left_side, right_side, preferred_element_type=F32)

    real_part = by_transpose(real_self, real_green) + by_transpose(imag_self, imag_green)
    imag_part = by_transpose(imag_self, real_green) - by_transpose(real_self, imag_green)
    product = jnp.stack([real_part, imag_part], axis=3).astype(BF16)
    y_piece = lax.all_gather(product, "freq", axis=0, tiled=True)
    real_piece = y_piece[:, :, :, 0]
    imag_piece = y_piece[:, :, :, 1]

    def plain_product(left_side, right_side):
        return jnp.einsum("esrm,mesk->esrk", left_side, right_side, preferred_element_type=F32)

    out_real = plain_product(real_rows, real_piece) - plain_product(imag_rows, imag_piece)
    out_imag = plain_product(real_rows, imag_piece) + plain_product(imag_rows, real_piece)
    return jnp.stack([out_real, out_imag], axis=2)


def by_rows(a, b):
    return lax.dot_general(a, b, (((1,), (1,)), ((), ())), preferred_element_type=F32)


def kernel(
    chunks, slabs, energies,
    lesser, retarded, coupling, numbers, shifts, beside_weight, out,
    own, low, high, c_buf, w_buf, r_buf, left_buf, acc, half, near, far, comb, result,
    store_sem, local_sem, send_sem, recv_sem,
):
    nf, size, _ = coupling.shape
    cut = size // chunks
    x, q, z = lax.axis_index("slab"), lax.axis_index("freq"), lax.axis_index("energy")
    y, core = q // 2, q % 2
    partner = {"freq": 2 * y + 1 - core}
    across = {"freq": 2 * (1 - y) + core}
    diagonal = {"freq": 2 * (1 - y) + 1 - core}
    opposite = {"slab": 1 - x}
    has_low, has_high = z > 0, z < energies - 1
    below = {"energy": jnp.maximum(z - 1, 0)}
    above = {"energy": jnp.minimum(z + 1, energies - 1)}
    x_to = x + 2 * core - 1
    has_x = jnp.logical_and(x_to >= 0, x_to < slabs)
    beside = {"slab": jnp.clip(x_to, 0, slabs - 1), "freq": 2 * y + 1 - core}

    barrier = pltpu.get_barrier_semaphore()
    peers = [(None, partner), (None, across), (None, diagonal), (None, opposite), (has_low, below), (has_high, above), (has_x, beside)]

    def under(condition, action):
        if condition is None:
            action()
        else:
            pl.when(condition)(action)

    for condition, peer in peers:
        under(condition, lambda peer=peer: pl.semaphore_signal(barrier, inc=1, device_id=peer, device_id_type=MESH))

    count = [0]

    def remote(src, dst, peer):
        n = count[0]
        count[0] += 1
        return pltpu.make_async_remote_copy(
            src_ref=src, dst_ref=dst, send_sem=send_sem.at[n], recv_sem=recv_sem.at[n],
            device_id=peer, device_id_type=MESH,
        )

    load_own = pltpu.make_async_copy(lesser.at[:, core, y], own, local_sem.at[0])
    load_c = [
        pltpu.make_async_copy(
            coupling.at[i, :, pl.ds(k * cut, cut)],
            c_buf.at[k, :, pl.ds(i * cut, cut)],
            local_sem.at[3 + i * chunks + k],
        )
        for i in range(nf)
        for k in range(chunks)
    ]
    load_r = pltpu.make_async_copy(retarded, r_buf, local_sem.at[1])
    for load in [load_own] + load_c:
        load.start()

    for i in range(nf):
        number, shift = numbers[i], shifts[i]
        none = jnp.float32(0.0)
        row = [
            jnp.where(shift == 1, number, none),
            jnp.where(shift == 2, number, none),
            jnp.where(shift == 1, number + 1.0, none),
            jnp.where(shift == 2, number + 1.0, none),
        ]
        for j in range(8):
            w_buf[i, j : j + 1, :] = jnp.full((1, cut), row[j % 4], F32)

    def zero(ref):
        ref[...] = jnp.zeros_like(ref)

    pl.when(jnp.logical_not(has_low))(lambda: zero(low))
    pl.when(jnp.logical_not(has_high))(lambda: zero(high))

    greeted = 4 + sum(condition.astype(jnp.int32) for condition in (has_low, has_high, has_x))
    pl.semaphore_wait(barrier, greeted)

    sent = []

    def go(copy, condition=None):
        under(condition, copy.start)
        sent.append((condition, copy))
        return copy

    w_in = [
        go(remote(w_buf.at[pl.ds(0, nf)], w_buf.at[pl.ds(slot * nf, nf)], peer))
        for slot, peer in ((1, partner), (2, across), (3, diagonal))
    ]

    def part(slot, k):
        start = slot * cut
        return c_buf.at[k, :, pl.ds(start if isinstance(start, int) else pl.multiple_of(start, cut), cut)]

    ups, downs, c_across, c_near = [], [], [], []
    for k in range(chunks):
        columns = pl.ds(k * cut, cut)
        c_across.append(go(remote(coupling.at[x, :, columns], part(2 * nf + x, k), across)))
    for k in range(chunks):
        columns = pl.ds(k * cut, cut)
        for i in range(nf):
            c_near.append(go(remote(coupling.at[i, :, columns], part(nf + i, k), partner)))
        ups.append(go(remote(lesser.at[:, core, y, :, columns], low.at[k], above), has_high))
        downs.append(go(remote(lesser.at[:, core, y, :, columns], high.at[k], below), has_low))

    load_r.start()
    load_own.wait()
    for load in load_c:
        load.wait()
    for copy in w_in:
        copy.wait_recv()

    def terms(k, e):
        columns = slice(k * cut, (k + 1) * cut)
        if e == 0:
            return low.at[k, 1], low.at[k, 0], own.at[1, :, columns], high.at[k, 0]
        return own.at[0, :, columns], low.at[k, 1], high.at[k, 0], high.at[k, 1]

    def left_side(k, e, number, slot_of):
        refs = terms(k, e)

        def body(j, carry):
            f = slot_of(j)
            w = w_buf[f]
            mixed = w[0:1] * refs[0][...].astype(F32)
            for i in (1, 2, 3):
                mixed = mixed + w[i : i + 1] * refs[i][...].astype(F32)
            columns = pl.ds(pl.multiple_of(f * cut, cut), cut)
            whole = jnp.concatenate([c_buf[h, :, columns] for h in range(chunks)], axis=1)
            left = jnp.dot(whole, mixed.astype(BF16), preferred_element_type=F32)
            left_buf[e, :, columns] = left.astype(BF16)
            return carry

        lax.fori_loop(0, number, body, 0, unroll=min(UNROLL, number))

    def right_side(k, e):
        return by_rows(left_buf[e], c_buf[k])

    def arrive(k):
        pl.when(has_low)(ups[k].wait_recv)
        pl.when(has_high)(downs[k].wait_recv)

    relayed, c_far = [], []
    for k in range(chunks):
        c_across[k].wait_recv()
        relayed.append(go(remote(part(2 * nf + x, k), part(2 * nf + x, k), opposite)))
        c_far.append(go(remote(part(2 * nf + x, k), part(3 * nf + x, k), partner)))
    arrive(0)
    for copy in c_near:
        copy.wait_recv()
    for e in range(2):
        left_side(0, e, 2 * nf, lambda j: j)
    other_x = 1 - x
    c_rest = []
    for k in range(chunks):
        relayed[k].wait_recv()
        c_rest.append(go(remote(part(2 * nf + other_x, k), part(3 * nf + other_x, k), partner)))
    for copy in c_far + c_rest:
        copy.wait_recv()
    for e in range(2):
        left_side(0, e, 2 * nf, lambda j: 2 * nf + j)
        acc[e] = right_side(0, e)

    for k in range(1, chunks - 1):
        arrive(k)
        for e in range(2):
            left_side(k, e, 4 * nf, lambda j: j)
            acc[e] += right_side(k, e)

    pairs = [(e, h) for e in range(2) for h in range(2)]
    to_far = {p: remote(half.at[p], far.at[p], beside) for p in pairs}
    to_near = {p: remote(half.at[p], near.at[p], partner) for p in pairs}
    comb_across = {(e, h): remote(comb.at[e, 0, h], comb.at[e, 2, h], across) for e, h in pairs}
    comb_near = {(e, h): remote(comb.at[e, 0, h], comb.at[e, 1, h], partner) for e, h in pairs}
    comb_far = {(e, h): remote(comb.at[e, 2, h], comb.at[e, 3, h], partner) for e, h in pairs}
    last = chunks - 1
    middle_column = size // 2

    def finish_self(e, h):
        columns = slice(h * middle_column, (h + 1) * middle_column)
        total = acc[e, :, columns] + by_rows(left_buf[e], c_buf[last, columns, :])
        half[e, h] = total.astype(BF16)
        go(to_far[e, h], has_x)
        go(to_near[e, h])

    def combine(e, h, with_far):
        to_near[e, h].wait_recv()
        around = near[e, h].astype(F32)
        if with_far:
            to_far[e, h].wait_recv()
            around = around + far[e, h].astype(F32)
        comb[e, 0, h] = (half[e, h].astype(F32) + beside_weight[core] * around).astype(BF16)
        comb_across[e, h].start()
        comb_near[e, h].start()

    alone = jnp.logical_not(has_x)

    def combine_alone(e, h):
        pl.when(alone)(lambda: combine(e, h, False))

    arrive(last)
    left_side(last, 0, 4 * nf, lambda j: j)
    finish_self(0, 0)
    finish_self(0, 1)
    combine_alone(0, 0)
    left_side(last, 1, 4 * nf, lambda j: j)
    combine_alone(0, 1)
    finish_self(1, 0)
    finish_self(1, 1)
    combine_alone(1, 0)
    combine_alone(1, 1)
    for e, h in pairs:
        pl.when(has_x)(lambda e=e, h=h: combine(e, h, True))

    load_r.wait()
    rows = size // 4
    mine = pl.ds(pl.multiple_of(q * rows, rows), rows)

    def pass_on(e):
        for h in range(2):
            comb_across[e, h].wait_recv()
            comb_far[e, h].start()

    def take(e):
        for h in range(2):
            comb_near[e, h].wait_recv()
            comb_far[e, h].wait_recv()

    def whole_sum(e, slot):
        return jnp.concatenate([comb[e, slot, 0], comb[e, slot, 1]], axis=1)

    stores = []

    for group in range(2):
        same = alone if group == 0 else has_x
        s = x if group == 0 else 1 - x
        other = jnp.where(same, 0, 1)
        for e in range(2):
            pl.when(same)(lambda e=e: pass_on(e))
            pl.when(jnp.logical_not(same))(lambda e=e: take(e))
            edge = jnp.concatenate([r_buf[e, s, 0, mine, :], r_buf[e, s, 1, mine, :]], axis=0)
            with_real = jnp.dot(edge, whole_sum(e, 2 * y + other), preferred_element_type=F32)
            with_imag = jnp.dot(edge, whole_sum(e, 2 * (1 - y) + other), preferred_element_type=F32)
            middle = jnp.concatenate(
                [with_real[:rows] - with_imag[rows:], with_imag[:rows] + with_real[rows:]], axis=0
            ).astype(BF16)
            by_real = by_rows(middle, r_buf[e, s, 0])
            by_imag = by_rows(middle, r_buf[e, s, 1])
            result[e, group, 0] = (by_real[:rows] + by_imag[rows:]).astype(BF16)
            result[e, group, 1] = (by_real[rows:] - by_imag[:rows]).astype(BF16)
            store = pltpu.make_async_copy(result.at[e, group], out.at[e, s], store_sem.at[e, group])
            store.start()
            stores.append(store)

    for copies in (comb_across, comb_near, comb_far):
        for p in pairs:
            copies[p].wait_send()
    for store in stores:
        store.wait()
    for condition, copy in sent:
        under(condition, copy.wait_send)


def fast(lesser, retarded, coupling, occupations, offsets, intersection):
    nf, size, _ = coupling.shape
    chunks = 2
    cut = size // chunks
    copies = 3 + (nf + 6) * chunks + 20
    anywhere = pl.BlockSpec(memory_space=pl.ANY)
    return pl.pallas_call(
        functools.partial(kernel, chunks, lax.axis_size("slab"), lax.axis_size("energy")),
        out_shape=jax.ShapeDtypeStruct((2, 2, 2, size // 4, size), BF16),
        in_specs=[anywhere] * 3 + [pl.BlockSpec(memory_space=pltpu.SMEM)] * 3,
        out_specs=anywhere,
        scratch_shapes=[
            pltpu.VMEM((2, size, size), BF16),
            pltpu.VMEM((chunks, 2, size, cut), BF16),
            pltpu.VMEM((chunks, 2, size, cut), BF16),
            pltpu.VMEM((chunks, size, 4 * nf * cut), BF16),
            pltpu.VMEM((4 * nf, 8, cut), F32),
            pltpu.VMEM((2, 2, 2, size, size), BF16),
            pltpu.VMEM((2, size, 4 * nf * cut), BF16),
            pltpu.VMEM((2, size, size), F32),
            pltpu.VMEM((2, 2, size, size // 2), BF16),
            pltpu.VMEM((2, 2, size, size // 2), BF16),
            pltpu.VMEM((2, 2, size, size // 2), BF16),
            pltpu.VMEM((2, 4, 2, size, size // 2), BF16),
            pltpu.VMEM((2, 2, 2, size // 4, size), BF16),
            pltpu.SemaphoreType.DMA((2, 2)),
            pltpu.SemaphoreType.DMA((3 + nf * chunks,)),
            pltpu.SemaphoreType.DMA((copies,)),
            pltpu.SemaphoreType.DMA((copies,)),
        ],
        compiler_params=pltpu.CompilerParams(
            collective_id=0, has_side_effects=True, vmem_limit_bytes=60 << 20
        ),
    )(lesser, retarded, coupling, occupations, offsets, intersection).astype(F32)


def solution(mesh):
    def shards(lesser, retarded, *rest):
        fits = (
            (mesh.shape["slab"], mesh.shape["freq"]) == (2, 4)
            and lesser.shape[:2] == (2, 2)
            and lesser.shape[-1] == 512
            and rest[0].shape[0] == 2
        )
        return (fast if fits else general)(lesser, retarded, *rest)

    return jax.shard_map(
        shards,
        mesh=mesh,
        in_specs=(
            P("energy", "slab", None, None, None),
            P("energy", "slab", None, None, None),
            P("freq", None, None),
            P("freq"),
            P("freq"),
            P("slab"),
        ),
        out_specs=P("energy", "slab", None, "freq", None),
        check_vma=False,
    )
```
